32 devices in a mesh: gx: 8 (over y, x, core), gy: 4 (over z).
Axes of the slice: x: 2, y: 2, z: 4, core: 2. Of those that a mesh axis runs over, the one named last changes fastest.
Arguments:
- state: bfloat16 [32, 12, 192, 256], P('gx', 'gy'), may hold values from -1 to 1
- weights: bfloat16 [32, 12, 9, 256, 256], P('gx', 'gy'), may hold values from -0.125 to 0.125
- drive: bfloat16 [2, 32, 12, 192, 256], P(None, 'gx', 'gy'), may hold values from -6 to 6
- leak: float32 [32, 12, 256], P('gx', 'gy'), may hold values from 0.1 to 1
- link_dev: int32 [8, 4, 12, 3], P(None, 'gy'), may hold values from 0 to 7, all different within a row; in each aligned block of 12 rows (0 to 11, 12 to 23, ..., all dimensions but the last counted through in order) at most 6 rows name the same one
- link_blk: int32 [8, 4, 12, 3], P(None, 'gy'), may hold values from 0 to 11
- offsets: int32 [5, 2], replicated, may hold values from -1 to 1, as said below
- gram_prev: float32 [32, 12, 256, 256], P('gx', 'gy'), may hold values from -6 to 6
Outputs:
- final_state: bfloat16 [32, 12, 192, 256], P('gx', 'gy')
- gram: float32 [32, 12, 256, 256], P('gx', 'gy')
The draws below stay inside these ranges and needn't reach their ends.
Inputs may be any that keep to these rules, and one draw needn't show every extreme that they name: `link_dev`: the 3 sources of one block lie on different indices of gx; among the blocks of one device at most 6 sources lie on any one index of gx, and exactly 6 on some. Five distinct offsets.
All inputs are finite; a program needn't handle non-finite values.
Results may differ from the reference program's by a relative error of at most 0.0046.
Values may be sent and summed in bfloat16 or wider, within the bound.
A program may use at most 192 MiB of HBM per device.

```python
import math
import jax
import jax.numpy as jnp
import numpy as np
from jax import lax

U = 256
LINKS = 3
STENCIL = 5
STEPS = 2
R = 4
C = 3
SEQ = 192
CAP = 6
NBR = 32
NBC = 12
N_GX = 8
N_GY = 4


def draw_offsets(key, part):
    chosen = jax.random.permutation(key, 9)[:STENCIL]
    return jnp.stack([chosen // 3 - 1, chosen % 3 - 1], axis=1).astype(jnp.int32)


def place_ends(drawn, stream_key, smallest, top_value):
    extent = drawn.shape
    place = [jax.random.randint(jax.random.fold_in(stream_key, axis), (), 0, extent[axis]) for axis in range(len(extent))]
    drawn = drawn.at[tuple(place)].set(smallest)
    longest = extent.index(max(extent))
    place[longest] = (place[longest] + 1) % extent[longest]
    return drawn.at[tuple(place)].set(top_value)


def levels(rng, extent, split, smallest, high):
    loudness, own = 1.0, jax.random.fold_in(rng, 6)
    for position, shards_of in split:
        steps = jnp.exp(jax.random.uniform(jax.random.fold_in(own, position), (shards_of,), jnp.float32, smallest / len(split), high / len(split)))
        loudness = loudness * jnp.repeat(steps, extent[position] // shards_of).reshape([-1 if axis == position else 1 for axis in range(len(extent))])
    return loudness


def routed_block(key, own, number, rows, number_of, top, most, slope):
    sequence = jax.random.permutation(key, number_of)
    packed, common = portions_of(number_of, rows * top, most, slope, True), portions_of(number_of, rows * top, most, slope, False)
    places = jnp.arange(number_of)

    def named(sizes, turn):
        used = int((sizes > 0).sum())
        fixed = max(1, used // 4)
        passed = fixed + (places - fixed + turn * (used - fixed)) % max(1, number_of - fixed)
        return jnp.zeros((number_of,), jnp.int32).at[sequence[jnp.where(places < fixed, places, passed)]].set(jnp.asarray(sizes, jnp.int32))

    sizes = jnp.where(number % 4 == 0, named(packed, number // 4), named(common, number - number // 4 - 1))
    mixed = jax.random.permutation(jax.random.fold_in(own, 3), number_of)
    giver, taker = mixed[0:number_of // 2 * 2:2], mixed[1:number_of // 2 * 2:2]
    room = jnp.minimum(sizes[giver] - 1, most - sizes[taker]) // 2
    room = jnp.where((giver == sequence[0]) | (taker == sequence[0]) | (sizes[taker] == 0), 0, jnp.maximum(room, 0))
    passed = jax.random.randint(jax.random.fold_in(own, 4), (number_of // 2,), 0, 1 << 20) % (room + 1)
    sizes = sizes.at[giver].add(-passed).at[taker].add(passed)
    labels = jnp.searchsorted(jnp.cumsum(sizes), jnp.arange(rows * top), side="right").astype(jnp.int32)
    listing = labels.reshape(top, rows).T
    listing = listing[jax.random.permutation(jax.random.fold_in(own, 1), rows)]
    turn = jax.random.randint(jax.random.fold_in(own, 2), (rows, 1), 0, top)
    return jnp.take_along_axis(listing, (jnp.arange(top)[None, :] + turn) % top, axis=1)


def portions_of(amount, total, limit, slope, full):
    loads = [(1 << 20) // math.isqrt(rank ** slope) + 1 for rank in range(1, amount + 1)]
    largest = limit if full else min(limit, max(-(-total // amount), total * loads[0] // sum(loads)))
    least = 1 if total - largest >= amount - 1 else 0
    counts, surplus = [largest] + [least] * (amount - 1), total - largest - least * (amount - 1)
    while surplus > 0:
        movable = [i for i in range(1, amount) if counts[i] < largest] or [i for i in range(1, amount) if counts[i] < limit]
        mass, budget = sum([loads[i] for i in movable]), surplus
        for i in movable:
            extra = min(limit - counts[i], max(1, budget * loads[i] // mass), surplus)
            counts[i] = counts[i] + extra
            surplus = surplus - extra
    return np.array(counts)


def bell_draw(stream_key, dims, spread, reach, split=(), kind=jnp.bfloat16):
    result = spread * jax.random.normal(stream_key, dims, jnp.float32)
    if split:
        result = result * levels(stream_key, dims, split, -0.22, 0.18)
    return jnp.clip(result, -reach, reach).astype(kind)


def setup_inputs(seed: int = 0) -> dict:
    keys = jax.random.split(jax.random.key(seed), 9)
    state = jnp.clip(jax.random.uniform(keys[0], (NBR, NBC, SEQ, U), jnp.float32, -1.0, 1.0) * levels(keys[0], (NBR, NBC, SEQ, U), ((0, 8), (1, 4)), -0.4, 0.0), -1.0, 1.0).astype(jnp.bfloat16)
    weights = bell_draw(keys[1], (NBR, NBC, STENCIL + LINKS + 1, U, U), ((STENCIL + LINKS + 1) * U) ** -0.5, 0.125, ((0, 8), (1, 4)))
    drive = bell_draw(keys[2], (STEPS, NBR, NBC, SEQ, U), 1.0, 6.0, ((1, 8), (2, 4)))
    leak = jnp.clip(jnp.exp(math.log(1.0) - 2.3025851 * jax.random.uniform(keys[3], (NBR, NBC, U), jnp.float32) ** levels(keys[3], (NBR, NBC, U), ((0, 8), (1, 4)), -0.2, 0.2)), 0.1, 1.0)
    link_dev_keys = jax.random.split(jax.random.fold_in(keys[4], 1), N_GX * N_GY * (R * C) // (R * C))
    link_dev_turns = jax.random.permutation(jax.random.fold_in(keys[4], 3), N_GX * N_GY * (R * C) // (R * C))
    link_dev = jax.vmap(lambda own, number: routed_block(jax.random.fold_in(keys[4], 2), own, number, R * C, N_GX, LINKS, CAP, 2))(link_dev_keys, link_dev_turns).reshape((N_GX, N_GY, R * C, LINKS))
    link_blk = place_ends(jax.random.randint(keys[5], (N_GX, N_GY, R * C, LINKS), 0, R * C), jax.random.fold_in(keys[5], 1), 0, (R * C) - 1).astype(jnp.int32)
    offsets = draw_offsets(jax.random.fold_in(keys[8], 71), 0)
    gram_prev = bell_draw(keys[7], (NBR, NBC, U, U), 1.0, 6.0, ((0, 8), (1, 4)), jnp.float32)
    return dict(state=state, weights=weights, drive=drive, leak=leak, link_dev=link_dev, link_blk=link_blk, offsets=offsets, gram_prev=gram_prev)


def reference(state, weights, drive, leak, link_dev, link_blk, offsets, gram_prev):
    dev_grid = link_dev.reshape(N_GX, N_GY, R, C, LINKS).transpose(0, 2, 1, 3, 4).reshape(NBR, NBC, LINKS)
    blk_grid = link_blk.reshape(N_GX, N_GY, R, C, LINKS).transpose(0, 2, 1, 3, 4).reshape(NBR, NBC, LINKS)
    col_band = (jnp.arange(NBC, dtype=jnp.int32) // C)[None, :, None]
    src_row = (dev_grid * R + blk_grid // C).astype(jnp.int32)
    src_col = (col_band * C + blk_grid % C).astype(jnp.int32)
    current = state
    gram = gram_prev
    for step_id in range(STEPS):
        padded = jnp.pad(current, ((1, 1), (1, 1), (0, 0), (0, 0)))

        def one_row(row_id):
            w_row = lax.dynamic_index_in_dim(weights, row_id, 0, keepdims=False)
            preact = jnp.zeros((NBC, SEQ, U), jnp.float32)
            for offset_id in range(STENCIL):
                start_r = (row_id + 1 + offsets[offset_id, 0]).astype(jnp.int32)
                start_c = (1 + offsets[offset_id, 1]).astype(jnp.int32)
                zero = jnp.zeros((), jnp.int32)
                nearby = lax.dynamic_slice(padded, (start_r, start_c, zero, zero), (1, NBC, SEQ, U))[0]
                preact = preact + jnp.einsum("csu,cuv->csv", nearby.astype(jnp.float32), w_row[:, offset_id].astype(jnp.float32))
            sources = current[src_row[row_id], src_col[row_id]]
            preact = preact + jnp.einsum("clsu,cluv->csv", sources.astype(jnp.float32), w_row[:, STENCIL:STENCIL + LINKS].astype(jnp.float32))
            inputs = lax.dynamic_index_in_dim(drive[step_id], row_id, 0, keepdims=False)
            preact = preact + jnp.einsum("csu,cuv->csv", inputs.astype(jnp.float32), w_row[:, STENCIL + LINKS].astype(jnp.float32))
            old_row = lax.dynamic_index_in_dim(current, row_id, 0, keepdims=False).astype(jnp.float32)
            rate = lax.dynamic_index_in_dim(leak, row_id, 0, keepdims=False)[:, None, :]
            fresh = ((1.0 - rate) * old_row + rate * jnp.tanh(preact)).astype(jnp.bfloat16)
            fresh_wide = fresh.astype(jnp.float32)
            return fresh, jnp.einsum("csu,csv->cuv", fresh_wide, fresh_wide)

        fresh_all, gram_terms = lax.map(one_row, jnp.arange(NBR, dtype=jnp.int32))
        current = fresh_all
        gram = gram + gram_terms
    return current, gram
```

```python
import functools

import jax
import jax.numpy as jnp
from jax import lax
from jax.experimental import pallas as pl
from jax.experimental.pallas import tpu as pltpu
from jax.sharding import PartitionSpec as P

MESH = pl.DeviceIdType.MESH
PART, ALONG_X, ALONG_Y, X_PART, Y_PART, DIAG, D_PART = range(7)


def padded(x, sides, width):
    for axis, dim in sides:
        size, length = (lax.axis_size(axis), x.shape[dim])
        up = [(i, (i + 1) % size) for i in range(size - 1)]
        down = [(j, i) for i, j in up]
        last = lax.slice_in_dim(x, length - width, length, axis=dim)
        first = lax.slice_in_dim(x, 0, width, axis=dim)
        before = lax.ppermute(last, axis, up)
        after = lax.ppermute(first, axis, down)
        x = jnp.concatenate([before, x, after], axis=dim)
    return x


def shards(state, weights, drive, leak, link_dev, link_blk, offsets, gram_prev):
    grid_rows, grid_cols, batch_cols, units = state.shape
    nblocks = grid_rows * grid_cols
    nlinks = link_dev.shape[-1]
    nstencil = offsets.shape[0]
    gx_size = lax.axis_size("gx")
    own_index = lax.axis_index("gx")
    all_dev = link_dev[:, 0].reshape(gx_size, nblocks * nlinks)
    all_blk = link_blk[:, 0].reshape(gx_size, nblocks * nlinks)
    my_dev = lax.dynamic_index_in_dim(all_dev, own_index, 0, keepdims=False)
    my_blk = lax.dynamic_index_in_dim(all_blk, own_index, 0, keepdims=False)
    w_long = weights[:, :, nstencil : nstencil + nlinks].reshape(nblocks, nlinks, units, units)
    current = state
    gram = gram_prev
    for step_id in range(drive.shape[0]):
        extended = padded(current, (("gx", 0), ("gy", 1)), 1)
        preact = jnp.zeros((grid_rows, grid_cols, batch_cols, units), jnp.float32)
        for offset_id in range(nstencil):
            zero = jnp.zeros((), jnp.int32)
            start_r = 1 + offsets[offset_id, 0]
            start_c = 1 + offsets[offset_id, 1]
            nearby = lax.dynamic_slice(
                extended, (start_r, start_c, zero, zero), (grid_rows, grid_cols, batch_cols, units)
            )
            preact = preact + jnp.einsum(
                "rcsu,rcuv->rcsv",
                nearby,
                weights[:, :, offset_id],
                preferred_element_type=jnp.float32,
            )
        flat_state = current.reshape(nblocks, batch_cols, units)
        whole = lax.all_gather(flat_state[None], "gx", axis=0, tiled=True)
        picked = whole.reshape(gx_size * nblocks, batch_cols, units)[my_dev * nblocks + my_blk]
        picked = picked.reshape(nblocks, nlinks, batch_cols, units)
        distant = jnp.einsum("blsu,bluv->bsv", picked, w_long, preferred_element_type=jnp.float32)
        preact = preact + distant.reshape(grid_rows, grid_cols, batch_cols, units)
        preact = preact + jnp.einsum(
            "rcsu,rcuv->rcsv",
            drive[step_id],
            weights[:, :, nstencil + nlinks],
            preferred_element_type=jnp.float32,
        )
        rate = leak[:, :, None, :]
        current = ((1.0 - rate) * current.astype(jnp.float32) + rate * jnp.tanh(preact)).astype(
            jnp.bfloat16
        )
        gram = gram + jnp.einsum(
            "rcsu,rcsv->rcuv", current, current, preferred_element_type=jnp.float32
        )
    return (current, gram)


def reservoir(
    n_gy, sizes, state, w, drive, leak, ldev, lblk, offs, gprev, out, gout, *scratch
):
    parts = len(sizes)
    phases = drive.shape[0] * parts
    last = phases - 1
    gaths, exts, rest = scratch[:phases], scratch[phases : 2 * phases], scratch[2 * phases :]
    wv, dv, gv, acc, xf, load_sem, store_sem, send_sem, recv_sem, zsend_sem, zrecv_sem = rest
    rows, cols, seq, units = state.shape
    nstencil, nlinks = offs.shape[1], ldev.shape[1]
    spans = [pl.ds(sum(sizes[: t % parts]), sizes[t % parts]) for t in range(phases)]
    g, b = lax.axis_index("gx"), lax.axis_index("gy")
    core, x, y = lax.rem(g, 2), lax.rem(lax.div(g, 2), 2), lax.div(g, 4)
    near = lambda fy, fx, fc: (
        (1 - y if fy else y) * 4 + (1 - x if fx else x) * 2 + (1 - core if fc else core)
    )
    ids = {
        PART: near(0, 0, 1), ALONG_X: near(0, 1, 0), ALONG_Y: near(1, 0, 0),
        X_PART: near(0, 1, 1), Y_PART: near(1, 0, 1), DIAG: near(1, 1, 0), D_PART: near(1, 1, 1),
    }
    has_left, has_right = b > 0, b < n_gy - 1
    has_up, has_down = g > 0, g < 7

    loads = []

    def load(src, dst):
        copy = pltpu.make_async_copy(src, dst, load_sem.at[len(loads)])
        copy.start()
        loads.append(copy)
        return copy

    for r in range(rows):
        for s in range(parts):
            load(state.at[r, :, spans[s]], gaths[s].at[g, pl.ds(r * cols, cols)])

    barrier = pltpu.get_barrier_semaphore()
    for rel in (PART, ALONG_X, ALONG_Y):
        pl.semaphore_signal(barrier, inc=1, device_id={"gx": ids[rel]}, device_id_type=MESH)

    @pl.when(has_left)
    def _():
        pl.semaphore_signal(barrier, inc=1, device_id={"gy": b - 1}, device_id_type=MESH)

    @pl.when(has_right)
    def _():
        pl.semaphore_signal(barrier, inc=1, device_id={"gy": b + 1}, device_id_type=MESH)

    inside = jnp.logical_and(has_left, has_right)

    @pl.when(inside)
    def _():
        pl.semaphore_wait(barrier, 5)

    @pl.when(jnp.logical_not(inside))
    def _():
        pl.semaphore_wait(barrier, 4 if n_gy > 1 else 3)

    sends = []

    def send(t, rel_from, r, to, rel_there):
        origin = g if rel_from is None else ids[rel_from]
        here = gaths[t].at[origin, pl.ds(r * cols, cols)]
        src = state.at[r, :, spans[t]] if rel_from is None and t < parts else here
        copy = pltpu.make_async_remote_copy(
            src_ref=src, dst_ref=here,
            send_sem=send_sem.at[len(sends)], recv_sem=recv_sem.at[t, rel_there, r],
            device_id={"gx": ids[to]}, device_id_type=MESH,
        )
        copy.start()
        sends.append(copy)

    def send_own(t, r, to):
        send(t, None, r, to, to)

    def arrived(t, rel, r):
        here = gaths[t].at[ids[rel], pl.ds(r * cols, cols)]
        pltpu.make_async_remote_copy(
            src_ref=here, dst_ref=here,
            send_sem=send_sem.at[0], recv_sem=recv_sem.at[t, rel, r],
            device_id={"gx": ids[PART]}, device_id_type=MESH,
        ).wait_recv()

    def relay(t, rel, r, across=None):
        arrived(t, rel, r)
        if across is not None:
            send(t, rel, r, across, DIAG)
        send(t, rel, r, PART, {ALONG_X: X_PART, ALONG_Y: Y_PART, DIAG: D_PART}[rel])

    def rim_copy(t, side, kind):
        col = 0 if side == 0 else cols - 1
        there = cols + 1 if side == 0 else 0
        gath, ext = gaths[t], exts[t]
        if kind == 0:
            return [
                pltpu.make_async_remote_copy(
                    src_ref=state.at[r, col, spans[t]]
                    if t < parts
                    else gath.at[g, r * cols + col],
                    dst_ref=ext.at[r + 1, there],
                    send_sem=zsend_sem.at[t, side, r], recv_sem=zrecv_sem.at[t, side, r],
                    device_id={"gy": b - 1 if side == 0 else b + 1}, device_id_type=MESH,
                )
                for r in range(rows)
            ]
        src = (
            gath.at[lax.rem(g + 7, 8), (rows - 1) * cols + col]
            if kind == 1
            else gath.at[lax.rem(g + 1, 8), col]
        )
        return [
            pltpu.make_async_remote_copy(
                src_ref=src,
                dst_ref=ext.at[0 if kind == 1 else rows + 1, there],
                send_sem=zsend_sem.at[t, side, rows + kind - 1],
                recv_sem=zrecv_sem.at[t, side, rows + kind - 1],
                device_id={"gy": b - 1 if side == 0 else b + 1}, device_id_type=MESH,
            )
        ]

    def rims(t, do, kinds):
        for side in (0, 1):
            present = (has_left, has_right)
            who = present[side] if do != "wait_recv" else present[1 - side]
            for kind in kinds:
                cond = who
                if kind == 1:
                    cond = jnp.logical_and(who, has_up)
                if kind == 2:
                    cond = jnp.logical_and(who, has_down)

                @pl.when(cond)
                def _():
                    for copy in rim_copy(t, side, kind):
                        getattr(copy, do)()

    def upfront(t):
        return 3 if t == last else 4

    def start(t):
        for x_row, y_row in ((0, 3), (3, 0), (1, 2), (2, 1))[: upfront(t)]:
            send_own(t, x_row, ALONG_X)
            send_own(t, y_row, ALONG_Y)
            send_own(t, x_row, PART)
        rims(t, "start", (0,))

    def exchange(t):
        relay(t, ALONG_X, 0, ALONG_Y)
        relay(t, ALONG_Y, 3, ALONG_X)
        for x_row, y_row in ((0, 3), (3, 0), (1, 2), (2, 1))[upfront(t) :]:
            send_own(t, x_row, ALONG_X)
            send_own(t, y_row, ALONG_Y)
            send_own(t, x_row, PART)
        relay(t, ALONG_Y, 0)
        relay(t, ALONG_X, 3)
        relay(t, ALONG_X, 1, ALONG_Y)
        relay(t, ALONG_Y, 2, ALONG_X)

    def borders(t):
        relay(t, DIAG, 0)
        relay(t, DIAG, 3)
        for rel in (PART, X_PART, D_PART):
            arrived(t, rel, 0)
            arrived(t, rel, 3)
        rims(t, "start", (1, 2))
        fill(t)
        rims(t, "wait_recv", (0, 1, 2))

    def finish(t):
        relay(t, ALONG_Y, 1)
        relay(t, ALONG_X, 2)
        relay(t, DIAG, 1)
        relay(t, DIAG, 2)
        for rel in (PART, X_PART, D_PART):
            arrived(t, rel, 1)
            arrived(t, rel, 2)
        for r in range(rows):
            arrived(t, Y_PART, r)

    def fill(t):
        gath, ext = gaths[t], exts[t]

        def place(i, carry):
            r, c = i // cols, lax.rem(i, cols)
            ext[r + 1, c + 1] = gath[g, i]
            return carry

        lax.fori_loop(0, rows * cols, place, 0)
        zero = jnp.zeros((sizes[t % parts], units), jnp.bfloat16)

        @pl.when(has_up)
        def _():
            for c in range(cols):
                ext[0, c + 1] = gath[lax.rem(g + 7, 8), (rows - 1) * cols + c]

        @pl.when(has_down)
        def _():
            for c in range(cols):
                ext[rows + 1, c + 1] = gath[lax.rem(g + 1, 8), c]

        for there, edge in ((0, has_up), (rows + 1, has_down)):

            @pl.when(jnp.logical_not(edge))
            def _():
                for c in range(cols + 2):
                    ext[there, c] = zero

        for there, side in ((0, has_left), (cols + 1, has_right)):

            @pl.when(jnp.logical_not(side))
            def _():
                for r in range(rows):
                    ext[r + 1, there] = zero
                for r, edge in ((0, has_up), (rows + 1, has_down)):

                    @pl.when(edge)
                    def _():
                        ext[r, there] = zero

    def dot(a, weight):
        return jnp.dot(a, weight, preferred_element_type=jnp.float32)

    def nearby(t):
        ext = exts[t]

        def one(i, carry):
            r, c = i // cols, lax.rem(i, cols)
            total = dot(dv[t // parts, r, c, spans[t]], wv[r, c, nstencil + nlinks])
            for k in range(nstencil):
                total = total + dot(ext[r + 1 + offs[0, k], c + 1 + offs[1, k]], wv[r, c, k])
            acc[i, pl.ds(0, sizes[t % parts])] = total
            return carry

        lax.fori_loop(0, rows * cols, one, 0, unroll=True)

    def gram_of(r, c, now):
        gv[r, c] += lax.dot_general(
            now, now, (((0,), (0,)), ((), ())), preferred_element_type=jnp.float32
        )

    def distant(t, r):
        gath = gaths[t]

        def one(c, carry):
            i = r * cols + c
            total = acc[i, pl.ds(0, sizes[t % parts])]
            for l in range(nlinks):
                total = total + dot(gath[ldev[g, l, 0, i], lblk[g, l, 0, i]], wv[r, c, nstencil + l])
            rate = leak[c, pl.ds(r, 1), :]
            old = gath[g, i].astype(jnp.float32)
            now = ((1.0 - rate) * old + rate * jnp.tanh(total)).astype(jnp.bfloat16)
            if t + parts >= phases:
                xf[i, spans[t]] = now
            else:
                gaths[t + parts][g, i] = now
                gram_of(r, c, now)
            return carry

        lax.fori_loop(0, cols, one, 0, unroll=True)

    stores = []

    def store(src, dst):
        copy = pltpu.make_async_copy(src, dst, store_sem.at[len(stores)])
        copy.start()
        stores.append(copy)

    start(0)
    for r in range(rows):
        load(w.at[r], wv.at[r])
    load(drive, dv)
    load(gprev, gv)
    for t in range(phases):
        exchange(t)
        if t < last:
            start(t + 1)
        if t == 0:
            for copy in loads:
                copy.wait()
        borders(t)
        nearby(t)
        finish(t)
        for r in range(rows):
            distant(t, r)
            if t == last:
                store(xf.at[pl.ds(r * cols, cols)], out.at[r])
        if t == phases - parts - 1:
            store(gv, gout)
    for copy in sends:
        copy.wait_send()
    for t in range(phases):
        rims(t, "wait_send", (0, 1, 2))
    for copy in stores:
        copy.wait()


def closing(x, gram, out, gout, xv, gv, x_sem, g_sem, out_sem, gout_sem):
    rows, cols = x.shape[:2]
    copy = pltpu.make_async_copy
    x_in = [copy(x.at[r], xv.at[r], x_sem.at[r]) for r in range(rows)]
    g_in = [copy(gram.at[r], gv.at[r], g_sem.at[r]) for r in range(rows)]
    x_out = [copy(xv.at[r], out.at[r], out_sem.at[r]) for r in range(rows)]
    g_out = [copy(gv.at[r], gout.at[r], gout_sem.at[r]) for r in range(rows)]
    for r in range(rows):
        x_in[r].start()
        g_in[r].start()
    for r in range(rows):
        x_in[r].wait()
        x_out[r].start()
        g_in[r].wait()
        for c in range(cols):
            now = xv[r, c]
            gv[r, c] += lax.dot_general(
                now, now, (((0,), (0,)), ((), ())), preferred_element_type=jnp.float32
            )
        g_out[r].start()
    for r in range(rows):
        x_out[r].wait()
        g_out[r].wait()


def fast_shards(n_gy, state, weights, drive, leak, link_dev, link_blk, offsets, gram_prev):
    rows, cols, seq, units = state.shape
    blocks = rows * cols
    steps = drive.shape[0]
    sizes = (96, 96)
    parts, phases = len(sizes), steps * len(sizes)
    anywhere = pl.BlockSpec(memory_space=pl.ANY)
    scalars = pl.BlockSpec(memory_space=pltpu.SMEM)
    last, gram = pl.pallas_call(
        functools.partial(reservoir, n_gy, sizes),
        out_shape=(
            jax.ShapeDtypeStruct(state.shape, state.dtype),
            jax.ShapeDtypeStruct(gram_prev.shape, gram_prev.dtype),
        ),
        in_specs=[
            anywhere, anywhere, anywhere, pl.BlockSpec(memory_space=pltpu.VMEM),
            scalars, scalars, scalars, anywhere,
        ],
        out_specs=(anywhere, anywhere),
        scratch_shapes=[
            *[pltpu.VMEM((8, blocks, m, units), jnp.bfloat16) for m in sizes] * steps,
            *[pltpu.VMEM((rows + 2, cols + 2, m, units), jnp.bfloat16) for m in sizes] * steps,
            pltpu.VMEM(weights.shape, weights.dtype),
            pltpu.VMEM(drive.shape, drive.dtype),
            pltpu.VMEM(gram_prev.shape, gram_prev.dtype),
            pltpu.VMEM((blocks, max(sizes), units), jnp.float32),
            pltpu.VMEM((blocks, seq, units), jnp.bfloat16),
            pltpu.SemaphoreType.DMA((rows * (parts + 1) + 2,)),
            pltpu.SemaphoreType.DMA((2 * rows,)),
            pltpu.SemaphoreType.DMA((28 * phases,)),
            pltpu.SemaphoreType.DMA((phases, 7, rows)),
            pltpu.SemaphoreType.DMA((phases, 2, rows + 2)),
            pltpu.SemaphoreType.DMA((phases, 2, rows + 2)),
        ],
        compiler_params=pltpu.CompilerParams(
            collective_id=0, has_side_effects=True, vmem_limit_bytes=62 * 1024 * 1024
        ),
    )(
        state, weights, drive, leak.transpose(1, 0, 2), link_dev.transpose(0, 3, 1, 2),
        link_blk.transpose(0, 3, 1, 2), offsets.T, gram_prev,
    )
    return pl.pallas_call(
        closing,
        out_shape=(
            jax.ShapeDtypeStruct(state.shape, state.dtype),
            jax.ShapeDtypeStruct(gram_prev.shape, gram_prev.dtype),
        ),
        in_specs=[anywhere, anywhere],
        out_specs=(anywhere, anywhere),
        scratch_shapes=[
            pltpu.VMEM(state.shape, state.dtype),
            pltpu.VMEM(gram_prev.shape, gram_prev.dtype),
            *[pltpu.SemaphoreType.DMA((rows,))] * 4,
        ],
        compiler_params=pltpu.CompilerParams(vmem_limit_bytes=62 * 1024 * 1024),
    )(last, gram)


def solution(mesh):
    part = shards
    if mesh.shape["gx"] == 8:
        part = functools.partial(fast_shards, mesh.shape["gy"])
    return jax.shard_map(
        part,
        mesh=mesh,
        in_specs=(
            P("gx", "gy", None, None),
            P("gx", "gy", None, None, None),
            P(None, "gx", "gy", None, None),
            P("gx", "gy", None),
            P(None, "gy", None, None),
            P(None, "gy", None, None),
            P(),
            P("gx", "gy", None, None),
        ),
        out_specs=(P("gx", "gy", None, None), P("gx", "gy", None, None)),
        check_vma=False,
    )
```
